512 devices in a mesh: bis: 128 (over z, y, x_lo), src: 4 (over x_hi, core).
Axes of the slice: x: 4 (x_hi: 2, x_lo: 2; x = x_hi * 2 + x_lo), y: 4, z: 16, core: 2. Of those that a mesh axis runs over, the one named last changes fastest.
Arguments:
- coefficients: float32 [4, 2, 64, 32768], P('src', None, None, 'bis'), may hold values from -6 to 6
- factors: float32 [4, 3, 2048, 64, 256], P('src', None, 'bis'), may hold values from -0.375 to 0.375
Outputs:
- potentials: float32 [2, 64, 32768], P(None, 'src', 'bis')
The draws below stay inside these ranges and needn't reach their ends.
All inputs are finite; a program needn't handle non-finite values.
Results may differ from the reference program's by a relative error of at most 0.0001.
Values sent between devices are 32-bit elements; how exact they have to be, the bound alone decides.
A program may use at most 64 MiB of HBM per device.

```python
import jax
import jax.numpy as jnp
from jax import lax

R = 64
NRHS = 16
LEVELS = 3
B_DEV = 16
S = 4
NB = 2048
N_BIS = 128


def steps_of(key, dims, shards, least, largest):
    def one(position, parts):
        heights = jax.random.uniform(jax.random.fold_in(jax.random.fold_in(key, 6), position), (parts,), jnp.float32, least / len(shards), largest / len(shards))
        return jnp.repeat(jnp.exp(heights), dims[position] // parts).reshape((-1,) + (1,) * (len(dims) - position - 1))

    loudness = one(*shards[0])
    for cut in shards[1:]:
        loudness = loudness * one(*cut)
    return loudness


def noise(stream_key, extent, deviation, bound, cuts=(), held_as=jnp.bfloat16):
    level = steps_of(stream_key, extent, cuts, -0.22, 0.18) if cuts else 1.0
    entries = jax.random.normal(stream_key, extent, jnp.float32) * deviation * level
    return jnp.minimum(jnp.maximum(entries, -bound), bound).astype(held_as)


def setup_inputs(seed: int = 0) -> dict:
    keys = jax.random.split(jax.random.key(seed), 3)
    coefficients = noise(keys[0], (S, 2, R, NB * NRHS), 1.0, 6.0, ((0, 4), (3, 128)), jnp.float32)
    factors = noise(keys[1], (S, LEVELS, NB, R, 4 * R), (4 * R) ** -0.5, 0.375, ((0, 4), (2, 128)), jnp.float32)
    return {"coefficients": coefficients, "factors": factors}


def mix_blocks(factor, stacked):
    return jnp.einsum("sboj,sjbk->sobk", factor, stacked, precision=lax.Precision.HIGHEST)


def reference(coefficients, factors):
    groups = coefficients.shape[0]
    state = coefficients.reshape(groups, 2, R, N_BIS * B_DEV, NRHS)
    middle = (N_BIS.bit_length() - 1) // 2
    for level_num in range(LEVELS):
        span = 2 ** (middle + 1 - level_num)
        shaped = state.reshape(groups, 2, R, N_BIS // (2 * span), 2, span * B_DEV, NRHS)
        partner = jnp.flip(shaped, 4).reshape(state.shape)
        stack_re = jnp.concatenate([state[:, 0], -state[:, 1], partner[:, 0], -partner[:, 1]], axis=1)
        stack_im = jnp.concatenate([state[:, 1], state[:, 0], partner[:, 1], partner[:, 0]], axis=1)
        factor = factors[:, level_num]
        state = jnp.stack([mix_blocks(factor, stack_re), mix_blocks(factor, stack_im)], axis=1)
    total = jnp.sum(state, axis=0)
    return total.reshape(2, R, N_BIS * B_DEV * NRHS)
```

```python
import functools

import jax
import jax.numpy as jnp
from jax import lax
from jax.experimental import pallas as pl
from jax.experimental.pallas import tpu as pltpu
from jax.sharding import PartitionSpec as P

LEVELS = 3
MESH = pl.DeviceIdType.MESH
LANES = 128


def flipped(index, step):
    return index + step - 2 * step * ((index // step) % 2)


def split(value):
    high = value.astype(jnp.bfloat16)
    low = (value - high.astype(jnp.float32)).astype(jnp.bfloat16)
    return high, low


def stacked(xr, xi, pr, pi):
    real = jnp.concatenate([xr, -xi, pr, -pi], axis=0)
    imag = jnp.concatenate([xi, xr, pi, pr], axis=0)
    return jnp.concatenate([real, imag], axis=1)


def kernel(steps, groups, rank, blocks, per_block,
           coef, fac, out,
           start, fbuf, fhigh, flow, recv, state, shares,
           coef_sem, fac_sem, send_sem, recv_sem, share_send, share_recv):
    halves = coef.shape[3] // LANES
    half_blocks = blocks // halves
    bis = lax.axis_index("bis")
    src = lax.axis_index("src")
    share = rank // groups
    partners = [flipped(bis, step) for step in steps]
    peers = []
    for k in range(1, groups):
        peer = src
        for bit in range(groups.bit_length() - 1):
            if (k >> bit) & 1:
                peer = flipped(peer, 1 << bit)
        peers.append(peer)

    coef_copy = pltpu.make_async_copy(coef.at[0], start, coef_sem)
    coef_copy.start()
    fac_copies = [
        pltpu.make_async_copy(fac.at[0, l], fbuf.at[l], fac_sem.at[l]) for l in range(LEVELS)
    ]
    for copy in fac_copies:
        copy.start()

    barrier = pltpu.get_barrier_semaphore()
    for partner in partners:
        pl.semaphore_signal(barrier, inc=1, device_id={"bis": partner}, device_id_type=MESH)
    for peer in peers:
        pl.semaphore_signal(barrier, inc=1, device_id={"src": peer}, device_id_type=MESH)
    pl.semaphore_wait(barrier, len(partners) + len(peers))

    def exchange(level, half):
        if level == 0:
            source = coef.at[0, :, :, pl.ds(half * LANES, LANES)]
        else:
            source = state.at[level - 1, half]
        return pltpu.make_async_remote_copy(
            src_ref=source,
            dst_ref=recv.at[level, half],
            send_sem=send_sem.at[level, half],
            recv_sem=recv_sem.at[level, half],
            device_id={"bis": partners[level]},
            device_id_type=MESH,
        )

    def share_copy(k, half):
        return pltpu.make_async_remote_copy(
            src_ref=state.at[LEVELS - 1, half, :, pl.ds(peers[k] * share, share), :],
            dst_ref=shares.at[k, half],
            send_sem=share_send.at[k, half],
            recv_sem=share_recv.at[k, half],
            device_id={"src": peers[k]},
            device_id_type=MESH,
        )

    for half in range(halves):
        exchange(0, half).start()
    for level in range(LEVELS):
        fac_copies[level].wait()
        high, low = split(fbuf[level])
        fhigh[level] = high
        flow[level] = low
    coef_copy.wait()

    lane_block = lax.broadcasted_iota(jnp.int32, (rank, 2 * LANES), 1) % LANES // per_block
    for level in range(LEVELS):
        for half in range(halves):
            copy = exchange(level, half)
            copy.wait_recv()
            if level == 0:
                own = start[:, :, half * LANES:(half + 1) * LANES]
            else:
                own = state[level - 1, half]
            other = recv[level, half]
            own_h, own_l = split(own)
            other_h, other_l = split(other)
            wh = stacked(own_h[0], own_h[1], other_h[0], other_h[1])
            wl = stacked(own_l[0], own_l[1], other_l[0], other_l[1])
            fh = fhigh[level, half * half_blocks:(half + 1) * half_blocks].reshape(half_blocks * rank, 4 * rank)
            fl = flow[level, half * half_blocks:(half + 1) * half_blocks].reshape(half_blocks * rank, 4 * rank)
            product = (
                jnp.dot(fh, wh, preferred_element_type=jnp.float32)
                + jnp.dot(fh, wl, preferred_element_type=jnp.float32)
                + jnp.dot(fl, wh, preferred_element_type=jnp.float32)
            )
            picked = product[0:rank]
            for b in range(1, half_blocks):
                picked = jnp.where(lane_block == b, product[b * rank:(b + 1) * rank], picked)
            state[level, half, 0] = picked[:, :LANES]
            state[level, half, 1] = picked[:, LANES:]
            if level + 1 < LEVELS:
                exchange(level + 1, half).start()
            else:
                for k in range(groups - 1):
                    share_copy(k, half).start()
    for half in range(halves):
        total = state[LEVELS - 1, half, :, pl.ds(pl.multiple_of(src * share, share), share), :]
        for k in range(groups - 1):
            share_copy(k, half).wait_recv()
            total = total + shares[k, half]
        out[:, :, half * LANES:(half + 1) * LANES] = total
    for level in range(LEVELS):
        for half in range(halves):
            exchange(level, half).wait_send()
    for half in range(halves):
        for k in range(groups - 1):
            share_copy(k, half).wait_send()


def per_device(coefficients, factors):
    middle = (lax.axis_size("bis").bit_length() - 1) // 2
    groups = lax.axis_size("src")
    _, _, rank, columns = coefficients.shape
    blocks = factors.shape[2]
    halves = columns // LANES
    share = rank // groups
    steps = [2 ** (middle + 1 - l) for l in range(LEVELS)]
    body = functools.partial(kernel, steps, groups, rank, blocks, columns // blocks)
    return pl.pallas_call(
        body,
        out_shape=jax.ShapeDtypeStruct((2, share, columns), jnp.float32),
        in_specs=[pl.BlockSpec(memory_space=pl.ANY)] * 2,
        out_specs=pl.BlockSpec(memory_space=pltpu.VMEM),
        scratch_shapes=[
            pltpu.VMEM((2, rank, columns), jnp.float32),
            pltpu.VMEM((LEVELS, blocks, rank, 4 * rank), jnp.float32),
            pltpu.VMEM((LEVELS, blocks, rank, 4 * rank), jnp.bfloat16),
            pltpu.VMEM((LEVELS, blocks, rank, 4 * rank), jnp.bfloat16),
            pltpu.VMEM((LEVELS, halves, 2, rank, LANES), jnp.float32),
            pltpu.VMEM((LEVELS, halves, 2, rank, LANES), jnp.float32),
            pltpu.VMEM((groups - 1, halves, 2, share, LANES), jnp.float32),
            pltpu.SemaphoreType.DMA,
            pltpu.SemaphoreType.DMA((LEVELS,)),
            pltpu.SemaphoreType.DMA((LEVELS, halves)),
            pltpu.SemaphoreType.DMA((LEVELS, halves)),
            pltpu.SemaphoreType.DMA((groups - 1, halves)),
            pltpu.SemaphoreType.DMA((groups - 1, halves)),
        ],
        compiler_params=pltpu.CompilerParams(
            collective_id=0, has_side_effects=True, vmem_limit_bytes=60 * 1024 * 1024
        ),
    )(coefficients, factors)


def solution(mesh):
    placed = (P("src", None, None, "bis"), P("src", None, "bis", None, None))
    return jax.shard_map(
        per_device, mesh=mesh, in_specs=placed, out_specs=P(None, "src", "bis"), check_vma=False
    )
```

```python
import functools

import jax
import jax.numpy as jnp
from jax import lax
from jax.experimental import pallas as pl
from jax.experimental.pallas import tpu as pltpu
from jax.sharding import PartitionSpec as P

LEVELS = 3
MESH = pl.DeviceIdType.MESH
LANES = 128
HALF = LANES // 2


def flipped(index, step):
    return index + step - 2 * step * ((index // step) % 2)


def turned(packed, low_half):
    moved = pltpu.roll(packed, HALF, 1)
    return jnp.where(low_half, -moved, moved)


def kernel(steps, groups, rank, blocks, per_block,
           coef, fac, out,
           start, fbuf, fsplit, first, recv, state, shares,
           coef_sem, fac_sem, first_sem, send_sem, recv_sem, share_send, share_recv, ready):
    chunks = blocks * per_block // HALF
    chunk_blocks = blocks // chunks
    rows = chunk_blocks * rank
    bis = lax.axis_index("bis")
    src = lax.axis_index("src")
    share = rank // groups
    partners = [flipped(bis, step) for step in steps]
    peers = []
    for k in range(1, groups):
        peer = src
        for bit in range(groups.bit_length() - 1):
            if (k >> bit) & 1:
                peer = flipped(peer, 1 << bit)
        peers.append(peer)

    coef_copy = pltpu.make_async_copy(coef.at[0], start, coef_sem)
    coef_copy.start()
    fac_copies = [
        pltpu.make_async_copy(fac.at[0, l], fbuf.at[l], fac_sem.at[l]) for l in range(LEVELS)
    ]
    for copy in fac_copies:
        copy.start()

    waits = [bis // steps[1] % 2, bis // steps[2] % 2]
    links = [{"bis": partners[1]}, {"bis": partners[2]}]
    for k in range(1, groups):
        waits.append(src // 2 % 2 if k >= 2 else 1 - src % 2)
        links.append({"src": peers[k - 1]})
    barrier = pltpu.get_barrier_semaphore()
    pl.semaphore_signal(barrier, inc=1, device_id={"bis": partners[0]}, device_id_type=MESH)
    for late, link in zip(waits, links):
        @pl.when(late == 0)
        def _(link=link):
            pl.semaphore_signal(barrier, inc=1, device_id=link, device_id_type=MESH)
    pl.semaphore_wait(barrier, 1 + sum(waits))

    def answered(i):
        @pl.when(waits[i] == 0)
        def _():
            pl.semaphore_wait(ready.at[i], 1)

    first_copy = pltpu.make_async_remote_copy(
        src_ref=coef.at[0, :, :, pl.ds(0, LANES)],
        dst_ref=first,
        send_sem=first_sem.at[0],
        recv_sem=first_sem.at[1],
        device_id={"bis": partners[0]},
        device_id_type=MESH,
    )
    first_copy.start()

    for i, (late, link) in enumerate(zip(waits, links)):
        @pl.when(late == 1)
        def _(i=i, link=link):
            pl.semaphore_signal(ready.at[i], inc=1, device_id=link, device_id_type=MESH)

    def exchange(level, chunk):
        return pltpu.make_async_remote_copy(
            src_ref=state.at[level, chunk],
            dst_ref=recv.at[level, chunk],
            send_sem=send_sem.at[level, chunk],
            recv_sem=recv_sem.at[level, chunk],
            device_id={"bis": partners[level]},
            device_id_type=MESH,
        )

    def share_copy(k, chunk):
        return pltpu.make_async_remote_copy(
            src_ref=state.at[LEVELS, chunk, pl.ds(pl.multiple_of(peers[k] * share, share), share), :],
            dst_ref=shares.at[k, chunk],
            send_sem=share_send.at[k, chunk],
            recv_sem=share_recv.at[k, chunk],
            device_id={"src": peers[k]},
            device_id_type=MESH,
        )

    low_half = lax.broadcasted_iota(jnp.int32, (rank, LANES), 1) < HALF
    lane_block = lax.broadcasted_iota(jnp.int32, (rank, LANES), 1) % HALF // per_block

    def packed(pair, chunk):
        real, imag = pair
        if chunk % 2 == 0:
            imag = pltpu.roll(imag, HALF, 1)
        else:
            real = pltpu.roll(real, HALF, 1)
        return jnp.where(low_half, real, imag)

    coef_copy.wait()
    for chunk in list(range(2, chunks)) + [0, 1]:
        tile = chunk // 2 * LANES
        state[0, chunk] = packed((start[0, :, tile:tile + LANES], start[1, :, tile:tile + LANES]), chunk)
        if chunk >= 2:
            exchange(0, chunk).start()

    for level in range(LEVELS):
        fac_copies[level].wait()

        def split_block(block, carry, level=level):
            value = fbuf[level, block]
            high = value.astype(jnp.bfloat16)
            low = (value - high.astype(jnp.float32)).astype(jnp.bfloat16)
            chunk = block // chunk_blocks
            row = pl.multiple_of(block % chunk_blocks * rank, rank)
            fsplit[level, chunk, pl.ds(row, rank), :] = high
            fsplit[level, chunk, pl.ds(row + rows, rank), :] = low
            return carry

        lax.fori_loop(0, blocks, split_block, 0)

    def step(level, chunk):
        own = state[level, chunk]
        if level == 0 and chunk < 2:
            if chunk == 0:
                first_copy.wait_recv()
            other = packed((first[0], first[1]), chunk)
        else:
            exchange(level, chunk).wait_recv()
            other = recv[level, chunk]
        weights = jnp.concatenate([own, turned(own, low_half), other, turned(other, low_half)], axis=0)
        high = weights.astype(jnp.bfloat16)
        low = (weights - high.astype(jnp.float32)).astype(jnp.bfloat16)
        fh = fsplit[level, chunk, :rows]
        fl = fsplit[level, chunk, rows:]
        product = jnp.dot(fh, jnp.concatenate([high, low], axis=1), preferred_element_type=jnp.float32)
        summed = product[:, :LANES] + product[:, LANES:] + jnp.dot(fl, high, preferred_element_type=jnp.float32)
        picked = summed[0:rank]
        for b in range(1, chunk_blocks):
            picked = jnp.where(lane_block == b, summed[b * rank:(b + 1) * rank], picked)
        state[level + 1, chunk] = picked
        if level + 1 < LEVELS:
            if chunk == 0:
                answered(level)
            exchange(level + 1, chunk).start()
        else:
            for k in range(groups - 1):
                if chunk == 0:
                    answered(LEVELS - 1 + k)
                share_copy(k, chunk).start()

    for level in range(LEVELS):
        for chunk in range(chunks):
            step(level, chunk)

    own_rows = pl.ds(pl.multiple_of(src * share, share), share)
    low_share = lax.broadcasted_iota(jnp.int32, (share, LANES), 1) < HALF
    for pair in range(chunks // 2):
        totals = []
        for chunk in (2 * pair, 2 * pair + 1):
            total = state[LEVELS, chunk, own_rows, :]
            for k in range(groups - 1):
                share_copy(k, chunk).wait_recv()
                total = total + shares[k, chunk]
            totals.append(total)
        tile = pair * LANES
        out[0, :, tile:tile + LANES] = jnp.where(low_share, totals[0], pltpu.roll(totals[1], HALF, 1))
        out[1, :, tile:tile + LANES] = jnp.where(low_share, pltpu.roll(totals[0], HALF, 1), totals[1])
    first_copy.wait_send()
    for level in range(LEVELS):
        for chunk in range(chunks):
            if level > 0 or chunk >= 2:
                exchange(level, chunk).wait_send()
    for chunk in range(chunks):
        for k in range(groups - 1):
            share_copy(k, chunk).wait_send()


def per_device(coefficients, factors):
    middle = (lax.axis_size("bis").bit_length() - 1) // 2
    groups = lax.axis_size("src")
    _, _, rank, columns = coefficients.shape
    blocks = factors.shape[2]
    chunks = columns // HALF
    share = rank // groups
    steps = [2 ** (middle + 1 - l) for l in range(LEVELS)]
    body = functools.partial(kernel, steps, groups, rank, blocks, columns // blocks)
    return pl.pallas_call(
        body,
        out_shape=jax.ShapeDtypeStruct((2, share, columns), jnp.float32),
        in_specs=[pl.BlockSpec(memory_space=pl.ANY)] * 2,
        out_specs=pl.BlockSpec(memory_space=pltpu.VMEM),
        scratch_shapes=[
            pltpu.VMEM((2, rank, columns), jnp.float32),
            pltpu.VMEM((LEVELS, blocks, rank, 4 * rank), jnp.float32),
            pltpu.VMEM((LEVELS, chunks, 2 * blocks // chunks * rank, 4 * rank), jnp.bfloat16),
            pltpu.VMEM((2, rank, LANES), jnp.float32),
            pltpu.VMEM((LEVELS, chunks, rank, LANES), jnp.float32),
            pltpu.VMEM((LEVELS + 1, chunks, rank, LANES), jnp.float32),
            pltpu.VMEM((groups - 1, chunks, share, LANES), jnp.float32),
            pltpu.SemaphoreType.DMA,
            pltpu.SemaphoreType.DMA((LEVELS,)),
            pltpu.SemaphoreType.DMA((2,)),
            pltpu.SemaphoreType.DMA((LEVELS, chunks)),
            pltpu.SemaphoreType.DMA((LEVELS, chunks)),
            pltpu.SemaphoreType.DMA((groups - 1, chunks)),
            pltpu.SemaphoreType.DMA((groups - 1, chunks)),
            pltpu.SemaphoreType.REGULAR((LEVELS + groups - 2,)),
        ],
        compiler_params=pltpu.CompilerParams(
            collective_id=0, has_side_effects=True, vmem_limit_bytes=56460000
        ),
    )(coefficients, factors)


def solution(mesh):
    placed = (P("src", None, None, "bis"), P("src", None, "bis", None, None))
    return jax.shard_map(
        per_device, mesh=mesh, in_specs=placed, out_specs=P(None, "src", "bis"), check_vma=False
    )
```

```python
import functools

import jax
import jax.numpy as jnp
from jax import lax
from jax.experimental import pallas as pl
from jax.experimental.pallas import tpu as pltpu
from jax.sharding import PartitionSpec as P

LEVELS = 3
MESH = pl.DeviceIdType.MESH
LANES = 128
HALF = LANES // 2


def flipped(index, step):
    return index + step - 2 * step * ((index // step) % 2)


def turned(packed, low_half):
    moved = pltpu.roll(packed, HALF, 1)
    return jnp.where(low_half, -moved, moved)


def kernel(steps, groups, rank, blocks, per_block,
           coef, fac, out,
           start, fbuf, fsplit, recv, state, shares,
           coef_sem, fac_sem, send_sem, recv_sem, share_send, share_recv, ready):
    chunks = blocks * per_block // HALF
    chunk_blocks = blocks // chunks
    rows = chunk_blocks * rank
    bis = lax.axis_index("bis")
    src = lax.axis_index("src")
    share = rank // groups
    partners = [flipped(bis, step) for step in steps]
    peers = []
    for k in range(1, groups):
        peer = src
        for bit in range(groups.bit_length() - 1):
            if (k >> bit) & 1:
                peer = flipped(peer, 1 << bit)
        peers.append(peer)

    coef_copies = []
    for half in range(chunks // 2):
        columns = pl.ds(half * LANES, LANES)
        coef_copies.append(pltpu.make_async_copy(coef.at[0, :, :, columns], start.at[:, :, columns], coef_sem.at[half]))
        coef_copies[-1].start()
    waits = [bis // steps[1] % 2, bis // steps[2] % 2]
    links = [{"bis": partners[1]}, {"bis": partners[2]}]
    for k in range(1, groups):
        waits.append(src // 2 % 2 if k >= 2 else 1 - src % 2)
        links.append({"src": peers[k - 1]})
    barrier = pltpu.get_barrier_semaphore()
    pl.semaphore_signal(barrier, inc=1, device_id={"bis": partners[0]}, device_id_type=MESH)
    for late, link in zip(waits, links):
        @pl.when(late == 0)
        def _(link=link):
            pl.semaphore_signal(barrier, inc=1, device_id=link, device_id_type=MESH)
    pl.semaphore_wait(barrier, 1 + sum(waits))

    def answered(i):
        @pl.when(waits[i] == 0)
        def _():
            pl.semaphore_wait(ready.at[i], 1)

    for i, (late, link) in enumerate(zip(waits, links)):
        @pl.when(late == 1)
        def _(i=i, link=link):
            pl.semaphore_signal(ready.at[i], inc=1, device_id=link, device_id_type=MESH)

    fac_copies = [
        pltpu.make_async_copy(fac.at[0, l], fbuf.at[l], fac_sem.at[l]) for l in range(LEVELS)
    ]
    for copy in fac_copies:
        copy.start()


    def exchange(level, chunk):
        return pltpu.make_async_remote_copy(
            src_ref=state.at[level, chunk],
            dst_ref=recv.at[level, chunk],
            send_sem=send_sem.at[level, chunk],
            recv_sem=recv_sem.at[level, chunk],
            device_id={"bis": partners[level]},
            device_id_type=MESH,
        )

    def share_copy(k, chunk):
        return pltpu.make_async_remote_copy(
            src_ref=state.at[LEVELS, chunk, pl.ds(pl.multiple_of(peers[k] * share, share), share), :],
            dst_ref=shares.at[k, chunk],
            send_sem=share_send.at[k, chunk],
            recv_sem=share_recv.at[k, chunk],
            device_id={"src": peers[k]},
            device_id_type=MESH,
        )

    low_half = lax.broadcasted_iota(jnp.int32, (rank, LANES), 1) < HALF
    lane_block = lax.broadcasted_iota(jnp.int32, (rank, LANES), 1) % HALF // per_block

    def packed(pair, chunk):
        real, imag = pair
        if chunk % 2 == 0:
            imag = pltpu.roll(imag, HALF, 1)
        else:
            real = pltpu.roll(real, HALF, 1)
        return jnp.where(low_half, real, imag)

    for chunk in range(chunks):
        tile = chunk // 2 * LANES
        if chunk % 2 == 0:
            coef_copies[chunk // 2].wait()
        state[0, chunk] = packed((start[0, :, tile:tile + LANES], start[1, :, tile:tile + LANES]), chunk)
        exchange(0, chunk).start()

    for level in range(LEVELS):
        fac_copies[level].wait()

        def split_block(block, carry, level=level):
            value = fbuf[level, block]
            high = value.astype(jnp.bfloat16)
            low = (value - high.astype(jnp.float32)).astype(jnp.bfloat16)
            chunk = block // chunk_blocks
            row = pl.multiple_of(block % chunk_blocks * rank, rank)
            fsplit[level, chunk, pl.ds(row, rank), :] = high
            fsplit[level, chunk, pl.ds(row + rows, rank), :] = low
            return carry

        lax.fori_loop(0, blocks, split_block, 0)

    def step(level, chunk):
        own = state[level, chunk]
        exchange(level, chunk).wait_recv()
        other = recv[level, chunk]
        weights = jnp.concatenate([own, turned(own, low_half), other, turned(other, low_half)], axis=0)
        high = weights.astype(jnp.bfloat16)
        low = (weights - high.astype(jnp.float32)).astype(jnp.bfloat16)
        fh = fsplit[level, chunk, :rows]
        fl = fsplit[level, chunk, rows:]
        product = jnp.dot(fh, jnp.concatenate([high, low], axis=1), preferred_element_type=jnp.float32)
        summed = product[:, :LANES] + product[:, LANES:] + jnp.dot(fl, high, preferred_element_type=jnp.float32)
        picked = summed[0:rank]
        for b in range(1, chunk_blocks):
            picked = jnp.where(lane_block == b, summed[b * rank:(b + 1) * rank], picked)
        state[level + 1, chunk] = picked
        if level + 1 < LEVELS:
            if chunk == 0:
                answered(level)
            exchange(level + 1, chunk).start()
        else:
            for k in range(groups - 1):
                if chunk == 0:
                    answered(LEVELS - 1 + k)
                share_copy(k, chunk).start()

    for level in range(LEVELS):
        for chunk in range(chunks):
            step(level, chunk)

    own_rows = pl.ds(pl.multiple_of(src * share, share), share)
    low_share = lax.broadcasted_iota(jnp.int32, (share, LANES), 1) < HALF
    for pair in range(chunks // 2):
        totals = []
        for chunk in (2 * pair, 2 * pair + 1):
            total = state[LEVELS, chunk, own_rows, :]
            for k in range(groups - 1):
                share_copy(k, chunk).wait_recv()
                total = total + shares[k, chunk]
            totals.append(total)
        tile = pair * LANES
        out[0, :, tile:tile + LANES] = jnp.where(low_share, totals[0], pltpu.roll(totals[1], HALF, 1))
        out[1, :, tile:tile + LANES] = jnp.where(low_share, pltpu.roll(totals[0], HALF, 1), totals[1])
    for level in range(LEVELS):
        for chunk in range(chunks):
            exchange(level, chunk).wait_send()
    for chunk in range(chunks):
        for k in range(groups - 1):
            share_copy(k, chunk).wait_send()


def per_device(coefficients, factors):
    middle = (lax.axis_size("bis").bit_length() - 1) // 2
    groups = lax.axis_size("src")
    _, _, rank, columns = coefficients.shape
    blocks = factors.shape[2]
    chunks = columns // HALF
    share = rank // groups
    steps = [2 ** (middle + 1 - l) for l in range(LEVELS)]
    body = functools.partial(kernel, steps, groups, rank, blocks, columns // blocks)
    return pl.pallas_call(
        body,
        out_shape=jax.ShapeDtypeStruct((2, share, columns), jnp.float32),
        in_specs=[pl.BlockSpec(memory_space=pl.ANY)] * 2,
        out_specs=pl.BlockSpec(memory_space=pltpu.VMEM),
        scratch_shapes=[
            pltpu.VMEM((2, rank, columns), jnp.float32),
            pltpu.VMEM((LEVELS, blocks, rank, 4 * rank), jnp.float32),
            pltpu.VMEM((LEVELS, chunks, 2 * blocks // chunks * rank, 4 * rank), jnp.bfloat16),
            pltpu.VMEM((LEVELS, chunks, rank, LANES), jnp.float32),
            pltpu.VMEM((LEVELS + 1, chunks, rank, LANES), jnp.float32),
            pltpu.VMEM((groups - 1, chunks, share, LANES), jnp.float32),
            pltpu.SemaphoreType.DMA((chunks // 2,)),
            pltpu.SemaphoreType.DMA((LEVELS,)),
            pltpu.SemaphoreType.DMA((LEVELS, chunks)),
            pltpu.SemaphoreType.DMA((LEVELS, chunks)),
            pltpu.SemaphoreType.DMA((groups - 1, chunks)),
            pltpu.SemaphoreType.DMA((groups - 1, chunks)),
            pltpu.SemaphoreType.REGULAR((LEVELS + groups - 2,)),
        ],
        compiler_params=pltpu.CompilerParams(
            collective_id=0, has_side_effects=True, vmem_limit_bytes=56460000
        ),
    )(coefficients, factors)


def solution(mesh):
    placed = (P("src", None, None, "bis"), P("src", None, "bis", None, None))
    return jax.shard_map(
        per_device, mesh=mesh, in_specs=placed, out_specs=P(None, "src", "bis"), check_vma=False
    )
```

```python
import functools

import jax
import jax.numpy as jnp
from jax import lax
from jax.experimental import pallas as pl
from jax.experimental.pallas import tpu as pltpu
from jax.sharding import PartitionSpec as P

LEVELS = 3
MESH = pl.DeviceIdType.MESH
LANES = 128
HALF = LANES // 2
MERGED = (2, 3)


def flipped(index, step):
    return index + step - 2 * step * ((index // step) % 2)


def turned(packed, low_half):
    moved = pltpu.roll(packed, HALF, 1)
    return jnp.where(low_half, -moved, moved)


def kernel(steps, groups, rank, blocks, per_block,
           coef, fac, out,
           start, fbuf, fsplit, recv, state, shares, far_factors, fmerged, far_state, far_shares,
           coef_sem, fac_sem, send_sem, recv_sem, share_send, share_recv, ready, factor_sem, far_send, far_recv):
    chunks = blocks * per_block // HALF
    chunk_blocks = blocks // chunks
    rows = chunk_blocks * rank
    bis = lax.axis_index("bis")
    src = lax.axis_index("src")
    share = rank // groups
    partners = [flipped(bis, step) for step in steps]
    peers = []
    for k in range(1, groups):
        peer = src
        for bit in range(groups.bit_length() - 1):
            if (k >> bit) & 1:
                peer = flipped(peer, 1 << bit)
        peers.append(peer)

    coef_copies = []
    for half in range(chunks // 2):
        columns = pl.ds(half * LANES, LANES)
        coef_copies.append(pltpu.make_async_copy(coef.at[0, :, :, columns], start.at[:, :, columns], coef_sem.at[half]))
        coef_copies[-1].start()
    waits = [bis // steps[1] % 2, bis // steps[2] % 2]
    links = [{"bis": partners[1]}, {"bis": partners[2]}]
    for k in range(1, groups):
        waits.append(src // 2 % 2 if k >= 2 else 1 - src % 2)
        links.append({"src": peers[k - 1]})
    for k in range(1, groups):
        waits.append(bis // steps[2] % 2)
        links.append({"bis": partners[2], "src": peers[k - 1]})
    def first_device(link):
        return jnp.logical_and(link.get("bis", bis) == 0, link.get("src", src) == 0)

    me_first = first_device({})
    waits = [
        jnp.where(me_first, 1, jnp.where(first_device(link), 0, late)) for late, link in zip(waits, links)
    ]
    barrier = pltpu.get_barrier_semaphore()
    pl.semaphore_signal(barrier, inc=1, device_id={"bis": partners[0]}, device_id_type=MESH)
    for late, link in zip(waits, links):
        @pl.when(late == 0)
        def _(link=link):
            pl.semaphore_signal(barrier, inc=1, device_id=link, device_id_type=MESH)
    pl.semaphore_wait(barrier, 1 + sum(waits))

    def answered(i):
        @pl.when(waits[i] == 0)
        def _():
            pl.semaphore_wait(ready.at[i], 1)

    for i, (late, link) in enumerate(zip(waits, links)):
        @pl.when(late == 1)
        def _(i=i, link=link):
            pl.semaphore_signal(ready.at[i], inc=1, device_id=link, device_id_type=MESH)

    fac_copies = [
        pltpu.make_async_copy(fac.at[0, l], fbuf.at[l], fac_sem.at[l]) for l in range(LEVELS)
    ]
    for copy in fac_copies:
        copy.start()


    def exchange(level, chunk):
        return pltpu.make_async_remote_copy(
            src_ref=state.at[level, chunk],
            dst_ref=recv.at[level, chunk],
            send_sem=send_sem.at[level, chunk],
            recv_sem=recv_sem.at[level, chunk],
            device_id={"bis": partners[level]},
            device_id_type=MESH,
        )

    def share_copy(k, chunk):
        return pltpu.make_async_remote_copy(
            src_ref=state.at[LEVELS, chunk, pl.ds(pl.multiple_of(peers[k] * share, share), share), :],
            dst_ref=shares.at[k, chunk],
            send_sem=share_send.at[k, chunk],
            recv_sem=share_recv.at[k, chunk],
            device_id={"src": peers[k]},
            device_id_type=MESH,
        )

    far_copies = []
    for chunk in MERGED:
        index = (chunk - MERGED[0]) * chunk_blocks
        far_copies.append(
            pltpu.make_async_remote_copy(
                src_ref=fac.at[0, LEVELS - 1, pl.ds(chunk * chunk_blocks, chunk_blocks), :, pl.ds(2 * rank, 2 * rank)],
                dst_ref=far_factors.at[pl.ds(index, chunk_blocks)],
                send_sem=factor_sem.at[0, chunk - MERGED[0]],
                recv_sem=factor_sem.at[1, chunk - MERGED[0]],
                device_id={"bis": partners[LEVELS - 1]},
                device_id_type=MESH,
            )
        )

    def far_share(k, chunk):
        peer = peers[k - 1] if k else src
        link = {"bis": partners[LEVELS - 1], "src": peer} if k else {"bis": partners[LEVELS - 1]}
        return pltpu.make_async_remote_copy(
            src_ref=far_state.at[chunk - MERGED[0], pl.ds(pl.multiple_of(peer * share, share), share), :],
            dst_ref=far_shares.at[k, chunk - MERGED[0]],
            send_sem=far_send.at[k, chunk - MERGED[0]],
            recv_sem=far_recv.at[k, chunk - MERGED[0]],
            device_id=link,
            device_id_type=MESH,
        )

    low_half = lax.broadcasted_iota(jnp.int32, (rank, LANES), 1) < HALF
    lane_block = lax.broadcasted_iota(jnp.int32, (rank, LANES), 1) % HALF // per_block

    def packed(pair, chunk):
        real, imag = pair
        if chunk % 2 == 0:
            imag = pltpu.roll(imag, HALF, 1)
        else:
            real = pltpu.roll(real, HALF, 1)
        return jnp.where(low_half, real, imag)

    for chunk in range(chunks):
        tile = chunk // 2 * LANES
        if chunk % 2 == 0:
            coef_copies[chunk // 2].wait()
        state[0, chunk] = packed((start[0, :, tile:tile + LANES], start[1, :, tile:tile + LANES]), chunk)
        exchange(0, chunk).start()

    @pl.when(waits[1] == 1)
    def _():
        for copy in far_copies:
            copy.start()


    for level in range(LEVELS):
        fac_copies[level].wait()

        def split_block(block, carry, level=level):
            value = fbuf[level, block]
            high = value.astype(jnp.bfloat16)
            low = (value - high.astype(jnp.float32)).astype(jnp.bfloat16)
            chunk = block // chunk_blocks
            row = pl.multiple_of(block % chunk_blocks * rank, rank)
            fsplit[level, chunk, pl.ds(row, rank), :] = high
            fsplit[level, chunk, pl.ds(row + rows, rank), :] = low
            return carry

        if level < LEVELS - 1:
            lax.fori_loop(0, blocks, split_block, 0)
        else:
            lax.fori_loop(0, MERGED[0] * chunk_blocks, split_block, 0)

    def split_merged(block, far):
        value = far_factors[block] if far else fbuf[LEVELS - 1, MERGED[0] * chunk_blocks + block, :, :2 * rank]
        high = value.astype(jnp.bfloat16)
        low = (value - high.astype(jnp.float32)).astype(jnp.bfloat16)
        chunk = block // chunk_blocks
        row = pl.multiple_of(block % chunk_blocks * rank, rank) + far * rows
        fmerged[chunk, pl.ds(row, rank), :] = high
        fmerged[chunk, pl.ds(row + 2 * rows, rank), :] = low

    def split_near(block, carry):
        split_merged(block, 0)
        return carry

    def split_far(block, carry):
        split_merged(block, 1)
        return carry

    lax.fori_loop(0, len(MERGED) * chunk_blocks, split_near, 0)

    def merged(chunk, value):
        index = chunk - MERGED[0]
        weights = jnp.concatenate([value, turned(value, low_half)], axis=0)
        high = weights.astype(jnp.bfloat16)
        low = (weights - high.astype(jnp.float32)).astype(jnp.bfloat16)
        product = jnp.dot(
            fmerged[index, :2 * rows], jnp.concatenate([high, low], axis=1), preferred_element_type=jnp.float32
        )
        summed = product[:, :LANES] + product[:, LANES:] + jnp.dot(
            fmerged[index, 2 * rows:], high, preferred_element_type=jnp.float32
        )
        for far in (1, 0):
            picked = summed[far * rows:far * rows + rank]
            for b in range(1, chunk_blocks):
                picked = jnp.where(lane_block == b, summed[far * rows + b * rank:far * rows + (b + 1) * rank], picked)
            if far:
                far_state[index] = picked
            else:
                state[LEVELS, chunk] = picked
        for k in range(groups):
            if chunk == MERGED[0] and k:
                answered(LEVELS - 1 + groups - 1 + k - 1)
            far_share(k, chunk).start()
        for k in range(groups - 1):
            if chunk == MERGED[0]:
                answered(LEVELS - 1 + k)
            share_copy(k, chunk).start()

    def step(level, chunk):
        own = state[level, chunk]
        exchange(level, chunk).wait_recv()
        other = recv[level, chunk]
        weights = jnp.concatenate([own, turned(own, low_half), other, turned(other, low_half)], axis=0)
        high = weights.astype(jnp.bfloat16)
        low = (weights - high.astype(jnp.float32)).astype(jnp.bfloat16)
        fh = fsplit[level, chunk, :rows]
        fl = fsplit[level, chunk, rows:]
        product = jnp.dot(fh, jnp.concatenate([high, low], axis=1), preferred_element_type=jnp.float32)
        summed = product[:, :LANES] + product[:, LANES:] + jnp.dot(fl, high, preferred_element_type=jnp.float32)
        picked = summed[0:rank]
        for b in range(1, chunk_blocks):
            picked = jnp.where(lane_block == b, summed[b * rank:(b + 1) * rank], picked)
        if level == LEVELS - 2 and chunk in MERGED:
            merged(chunk, picked)
            return
        state[level + 1, chunk] = picked
        if level + 1 < LEVELS:
            if chunk == 0 and level == 0:
                answered(0)
            exchange(level + 1, chunk).start()
        else:
            for k in range(groups - 1):
                share_copy(k, chunk).start()

    for level in range(LEVELS):
        for chunk in range(chunks if level < LEVELS - 1 else MERGED[0]):
            if level == LEVELS - 2 and chunk in MERGED:
                index = chunk - MERGED[0]
                far_copies[index].wait_recv()
                lax.fori_loop(index * chunk_blocks, (index + 1) * chunk_blocks, split_far, 0)
            step(level, chunk)
            if level == 0 and chunk == 0:
                @pl.when(waits[1] == 0)
                def _():
                    pl.semaphore_wait(ready.at[1], 1)
                    for copy in far_copies:
                        copy.start()

    own_rows = pl.ds(pl.multiple_of(src * share, share), share)
    low_share = lax.broadcasted_iota(jnp.int32, (share, LANES), 1) < HALF
    for pair in range(chunks // 2):
        totals = []
        for chunk in (2 * pair, 2 * pair + 1):
            total = state[LEVELS, chunk, own_rows, :]
            for k in range(groups - 1):
                share_copy(k, chunk).wait_recv()
                total = total + shares[k, chunk]
            if chunk in MERGED:
                for k in range(groups):
                    far_share(k, chunk).wait_recv()
                    total = total + far_shares[k, chunk - MERGED[0]]
            totals.append(total)
        tile = pair * LANES
        out[0, :, tile:tile + LANES] = jnp.where(low_share, totals[0], pltpu.roll(totals[1], HALF, 1))
        out[1, :, tile:tile + LANES] = jnp.where(low_share, pltpu.roll(totals[0], HALF, 1), totals[1])
    for level in range(LEVELS):
        for chunk in range(chunks):
            if level < LEVELS - 1 or chunk not in MERGED:
                exchange(level, chunk).wait_send()
    for copy in far_copies:
        copy.wait_send()
    for chunk in MERGED:
        for k in range(groups):
            far_share(k, chunk).wait_send()
    for chunk in range(chunks):
        for k in range(groups - 1):
            share_copy(k, chunk).wait_send()


def per_device(coefficients, factors):
    middle = (lax.axis_size("bis").bit_length() - 1) // 2
    groups = lax.axis_size("src")
    _, _, rank, columns = coefficients.shape
    blocks = factors.shape[2]
    chunks = columns // HALF
    share = rank // groups
    steps = [2 ** (middle + 1 - l) for l in range(LEVELS)]
    body = functools.partial(kernel, steps, groups, rank, blocks, columns // blocks)
    return pl.pallas_call(
        body,
        out_shape=jax.ShapeDtypeStruct((2, share, columns), jnp.float32),
        in_specs=[pl.BlockSpec(memory_space=pl.ANY)] * 2,
        out_specs=pl.BlockSpec(memory_space=pltpu.VMEM),
        scratch_shapes=[
            pltpu.VMEM((2, rank, columns), jnp.float32),
            pltpu.VMEM((LEVELS, blocks, rank, 4 * rank), jnp.float32),
            pltpu.VMEM((LEVELS, chunks, 2 * blocks // chunks * rank, 4 * rank), jnp.bfloat16),
            pltpu.VMEM((LEVELS, chunks, rank, LANES), jnp.float32),
            pltpu.VMEM((LEVELS + 1, chunks, rank, LANES), jnp.float32),
            pltpu.VMEM((groups - 1, chunks, share, LANES), jnp.float32),
            pltpu.VMEM((len(MERGED) * blocks // chunks, rank, 2 * rank), jnp.float32),
            pltpu.VMEM((len(MERGED), 4 * blocks // chunks * rank, 2 * rank), jnp.bfloat16),
            pltpu.VMEM((len(MERGED), rank, LANES), jnp.float32),
            pltpu.VMEM((groups, len(MERGED), share, LANES), jnp.float32),
            pltpu.SemaphoreType.DMA((chunks // 2,)),
            pltpu.SemaphoreType.DMA((LEVELS,)),
            pltpu.SemaphoreType.DMA((LEVELS, chunks)),
            pltpu.SemaphoreType.DMA((LEVELS, chunks)),
            pltpu.SemaphoreType.DMA((groups - 1, chunks)),
            pltpu.SemaphoreType.DMA((groups - 1, chunks)),
            pltpu.SemaphoreType.REGULAR((LEVELS - 1 + 2 * (groups - 1),)),
            pltpu.SemaphoreType.DMA((2, len(MERGED))),
            pltpu.SemaphoreType.DMA((groups, len(MERGED))),
            pltpu.SemaphoreType.DMA((groups, len(MERGED))),
        ],
        compiler_params=pltpu.CompilerParams(
            collective_id=0, has_side_effects=True, vmem_limit_bytes=56460000
        ),
    )(coefficients, factors)


def solution(mesh):
    placed = (P("src", None, None, "bis"), P("src", None, "bis", None, None))
    return jax.shard_map(
        per_device, mesh=mesh, in_specs=placed, out_specs=P(None, "src", "bis"), check_vma=False
    )
```

```python
import functools

import jax
import jax.numpy as jnp
from jax import lax
from jax.experimental import pallas as pl
from jax.experimental.pallas import tpu as pltpu
from jax.sharding import PartitionSpec as P

LEVELS = 3
MESH = pl.DeviceIdType.MESH
LANES = 128
HALF = LANES // 2
MERGED = (2, 3)


def flipped(index, step):
    return index + step - 2 * step * ((index // step) % 2)


def turned(packed, low_half):
    moved = pltpu.roll(packed, HALF, 1)
    return jnp.where(low_half, -moved, moved)


def kernel(steps, groups, rank, blocks, per_block,
           coef, fac, out,
           start, fbuf, fsplit, recv, state, shares, far_factors, fmerged, far_state, far_shares,
           coef_sem, fac_sem, send_sem, recv_sem, share_send, share_recv, ready, factor_sem, far_send, far_recv):
    chunks = blocks * per_block // HALF
    chunk_blocks = blocks // chunks
    rows = chunk_blocks * rank
    bis = lax.axis_index("bis")
    src = lax.axis_index("src")
    share = rank // groups
    partners = [flipped(bis, step) for step in steps]
    peers = []
    for k in range(1, groups):
        peer = src
        for bit in range(groups.bit_length() - 1):
            if (k >> bit) & 1:
                peer = flipped(peer, 1 << bit)
        peers.append(peer)

    coef_copies = []
    for half in range(chunks // 2):
        columns = pl.ds(half * LANES, LANES)
        coef_copies.append(pltpu.make_async_copy(coef.at[0, :, :, columns], start.at[:, :, columns], coef_sem.at[half]))
        coef_copies[-1].start()
    waits = [bis // steps[1] % 2, bis // steps[2] % 2]
    links = [{"bis": partners[1]}, {"bis": partners[2]}]
    for k in range(1, groups):
        waits.append(src // 2 % 2 if k >= 2 else 1 - src % 2)
        links.append({"src": peers[k - 1]})
    for k in range(1, groups):
        waits.append(bis // steps[2] % 2)
        links.append({"bis": partners[2], "src": peers[k - 1]})
    def first_device(link):
        return jnp.logical_and(link.get("bis", bis) == 0, link.get("src", src) == 0)

    me_first = first_device({})
    waits = [
        jnp.where(me_first, 1, jnp.where(first_device(link), 0, late)) for late, link in zip(waits, links)
    ]
    barrier = pltpu.get_barrier_semaphore()
    pl.semaphore_signal(barrier, inc=1, device_id={"bis": partners[0]}, device_id_type=MESH)
    for late, link in zip(waits, links):
        @pl.when(late == 0)
        def _(link=link):
            pl.semaphore_signal(barrier, inc=1, device_id=link, device_id_type=MESH)
    pl.semaphore_wait(barrier, 1 + sum(waits))

    def answered(i):
        @pl.when(waits[i] == 0)
        def _():
            pl.semaphore_wait(ready.at[i], 1)

    for i, (late, link) in enumerate(zip(waits, links)):
        @pl.when(late == 1)
        def _(i=i, link=link):
            pl.semaphore_signal(ready.at[i], inc=1, device_id=link, device_id_type=MESH)

    fac_copies = [
        pltpu.make_async_copy(fac.at[0, l], fbuf.at[l], fac_sem.at[l]) for l in range(LEVELS)
    ]
    for copy in fac_copies:
        copy.start()


    def exchange(level, chunk):
        return pltpu.make_async_remote_copy(
            src_ref=state.at[level, chunk],
            dst_ref=recv.at[level, chunk],
            send_sem=send_sem.at[level, chunk],
            recv_sem=recv_sem.at[level, chunk],
            device_id={"bis": partners[level]},
            device_id_type=MESH,
        )

    def share_copy(k, chunk):
        return pltpu.make_async_remote_copy(
            src_ref=state.at[LEVELS, chunk, pl.ds(pl.multiple_of(peers[k] * share, share), share), :],
            dst_ref=shares.at[k, chunk],
            send_sem=share_send.at[k, chunk],
            recv_sem=share_recv.at[k, chunk],
            device_id={"src": peers[k]},
            device_id_type=MESH,
        )

    far_copies = []
    for chunk in MERGED:
        index = (chunk - MERGED[0]) * chunk_blocks
        far_copies.append(
            pltpu.make_async_remote_copy(
                src_ref=fac.at[0, LEVELS - 1, pl.ds(chunk * chunk_blocks, chunk_blocks), :, pl.ds(2 * rank, 2 * rank)],
                dst_ref=far_factors.at[pl.ds(index, chunk_blocks)],
                send_sem=factor_sem.at[0, chunk - MERGED[0]],
                recv_sem=factor_sem.at[1, chunk - MERGED[0]],
                device_id={"bis": partners[LEVELS - 1]},
                device_id_type=MESH,
            )
        )

    def far_share(k, chunk):
        peer = peers[k - 1] if k else src
        link = {"bis": partners[LEVELS - 1], "src": peer} if k else {"bis": partners[LEVELS - 1]}
        return pltpu.make_async_remote_copy(
            src_ref=far_state.at[chunk - MERGED[0], pl.ds(pl.multiple_of(peer * share, share), share), :],
            dst_ref=far_shares.at[k, chunk - MERGED[0]],
            send_sem=far_send.at[k, chunk - MERGED[0]],
            recv_sem=far_recv.at[k, chunk - MERGED[0]],
            device_id=link,
            device_id_type=MESH,
        )

    low_half = lax.broadcasted_iota(jnp.int32, (rank, LANES), 1) < HALF
    lane_block = lax.broadcasted_iota(jnp.int32, (rank, LANES), 1) % HALF // per_block

    def packed(pair, chunk):
        real, imag = pair
        if chunk % 2 == 0:
            imag = pltpu.roll(imag, HALF, 1)
        else:
            real = pltpu.roll(real, HALF, 1)
        return jnp.where(low_half, real, imag)

    for chunk in range(chunks):
        tile = chunk // 2 * LANES
        if chunk % 2 == 0:
            coef_copies[chunk // 2].wait()
        state[0, chunk] = packed((start[0, :, tile:tile + LANES], start[1, :, tile:tile + LANES]), chunk)
        exchange(0, chunk).start()

    @pl.when(waits[1] == 1)
    def _():
        for copy in far_copies:
            copy.start()


    for level in range(LEVELS):
        fac_copies[level].wait()

        def split_block(block, carry, level=level):
            value = fbuf[level, block]
            high = value.astype(jnp.bfloat16)
            low = (value - high.astype(jnp.float32)).astype(jnp.bfloat16)
            chunk = block // chunk_blocks
            row = pl.multiple_of(block % chunk_blocks * rank, rank)
            fsplit[level, chunk, pl.ds(row, rank), :] = high
            fsplit[level, chunk, pl.ds(row + rows, rank), :] = low
            return carry

        if level < LEVELS - 1:
            lax.fori_loop(0, blocks, split_block, 0)
        else:
            lax.fori_loop(0, MERGED[0] * chunk_blocks, split_block, 0)

    def split_merged(block, far):
        value = far_factors[block] if far else fbuf[LEVELS - 1, MERGED[0] * chunk_blocks + block, :, :2 * rank]
        high = value.astype(jnp.bfloat16)
        low = (value - high.astype(jnp.float32)).astype(jnp.bfloat16)
        chunk = block // chunk_blocks
        row = pl.multiple_of(block % chunk_blocks * rank, rank) + far * rows
        fmerged[chunk, pl.ds(row, rank), :] = high
        fmerged[chunk, pl.ds(row + 2 * rows, rank), :] = low

    def split_near(block, carry):
        split_merged(block, 0)
        return carry

    def split_far(block, carry):
        split_merged(block, 1)
        return carry

    lax.fori_loop(0, len(MERGED) * chunk_blocks, split_near, 0)

    def merged(chunk, value):
        index = chunk - MERGED[0]
        weights = jnp.concatenate([value, turned(value, low_half)], axis=0)
        high = weights.astype(jnp.bfloat16)
        low = (weights - high.astype(jnp.float32)).astype(jnp.bfloat16)
        stacked = jnp.concatenate([high, low], axis=1)
        for far in (1, 0):
            base = far * rows
            product = jnp.dot(fmerged[index, base:base + rows], stacked, preferred_element_type=jnp.float32)
            summed = product[:, :LANES] + product[:, LANES:] + jnp.dot(
                fmerged[index, 2 * rows + base:3 * rows + base], high, preferred_element_type=jnp.float32
            )
            picked = summed[:rank]
            for b in range(1, chunk_blocks):
                picked = jnp.where(lane_block == b, summed[b * rank:(b + 1) * rank], picked)
            if far:
                far_state[index] = picked
                for k in reversed(range(groups)):
                    if chunk == MERGED[0] and k:
                        answered(LEVELS - 1 + groups - 1 + k - 1)
                    far_share(k, chunk).start()
            else:
                state[LEVELS, chunk] = picked
                for k in range(groups - 1):
                    if chunk == MERGED[0]:
                        answered(LEVELS - 1 + k)
                    share_copy(k, chunk).start()

    def step(level, chunk):
        own = state[level, chunk]
        exchange(level, chunk).wait_recv()
        other = recv[level, chunk]
        weights = jnp.concatenate([own, turned(own, low_half), other, turned(other, low_half)], axis=0)
        high = weights.astype(jnp.bfloat16)
        low = (weights - high.astype(jnp.float32)).astype(jnp.bfloat16)
        fh = fsplit[level, chunk, :rows]
        fl = fsplit[level, chunk, rows:]
        product = jnp.dot(fh, jnp.concatenate([high, low], axis=1), preferred_element_type=jnp.float32)
        summed = product[:, :LANES] + product[:, LANES:] + jnp.dot(fl, high, preferred_element_type=jnp.float32)
        picked = summed[0:rank]
        for b in range(1, chunk_blocks):
            picked = jnp.where(lane_block == b, summed[b * rank:(b + 1) * rank], picked)
        if level == LEVELS - 2 and chunk in MERGED:
            merged(chunk, picked)
            return
        state[level + 1, chunk] = picked
        if level + 1 < LEVELS:
            if chunk == 0 and level == 0:
                answered(0)
            exchange(level + 1, chunk).start()
        else:
            for k in range(groups - 1):
                share_copy(k, chunk).start()

    for level in range(LEVELS):
        for chunk in range(chunks if level < LEVELS - 1 else MERGED[0]):
            if level == LEVELS - 2 and chunk in MERGED:
                index = chunk - MERGED[0]
                far_copies[index].wait_recv()
                lax.fori_loop(index * chunk_blocks, (index + 1) * chunk_blocks, split_far, 0)
            step(level, chunk)
            if level == 0 and chunk == 0:
                @pl.when(waits[1] == 0)
                def _():
                    pl.semaphore_wait(ready.at[1], 1)
                    for copy in far_copies:
                        copy.start()

    own_rows = pl.ds(pl.multiple_of(src * share, share), share)
    low_share = lax.broadcasted_iota(jnp.int32, (share, LANES), 1) < HALF
    for pair in range(chunks // 2):
        totals = []
        for chunk in (2 * pair, 2 * pair + 1):
            total = state[LEVELS, chunk, own_rows, :]
            for k in range(groups - 1):
                share_copy(k, chunk).wait_recv()
                total = total + shares[k, chunk]
            if chunk in MERGED:
                for k in range(groups):
                    far_share(k, chunk).wait_recv()
                    total = total + far_shares[k, chunk - MERGED[0]]
            totals.append(total)
        tile = pair * LANES
        out[0, :, tile:tile + LANES] = jnp.where(low_share, totals[0], pltpu.roll(totals[1], HALF, 1))
        out[1, :, tile:tile + LANES] = jnp.where(low_share, pltpu.roll(totals[0], HALF, 1), totals[1])
    for level in range(LEVELS):
        for chunk in range(chunks):
            if level < LEVELS - 1 or chunk not in MERGED:
                exchange(level, chunk).wait_send()
    for copy in far_copies:
        copy.wait_send()
    for chunk in MERGED:
        for k in range(groups):
            far_share(k, chunk).wait_send()
    for chunk in range(chunks):
        for k in range(groups - 1):
            share_copy(k, chunk).wait_send()


def per_device(coefficients, factors):
    middle = (lax.axis_size("bis").bit_length() - 1) // 2
    groups = lax.axis_size("src")
    _, _, rank, columns = coefficients.shape
    blocks = factors.shape[2]
    chunks = columns // HALF
    share = rank // groups
    steps = [2 ** (middle + 1 - l) for l in range(LEVELS)]
    body = functools.partial(kernel, steps, groups, rank, blocks, columns // blocks)
    return pl.pallas_call(
        body,
        out_shape=jax.ShapeDtypeStruct((2, share, columns), jnp.float32),
        in_specs=[pl.BlockSpec(memory_space=pl.ANY)] * 2,
        out_specs=pl.BlockSpec(memory_space=pltpu.VMEM),
        scratch_shapes=[
            pltpu.VMEM((2, rank, columns), jnp.float32),
            pltpu.VMEM((LEVELS, blocks, rank, 4 * rank), jnp.float32),
            pltpu.VMEM((LEVELS, chunks, 2 * blocks // chunks * rank, 4 * rank), jnp.bfloat16),
            pltpu.VMEM((LEVELS, chunks, rank, LANES), jnp.float32),
            pltpu.VMEM((LEVELS + 1, chunks, rank, LANES), jnp.float32),
            pltpu.VMEM((groups - 1, chunks, share, LANES), jnp.float32),
            pltpu.VMEM((len(MERGED) * blocks // chunks, rank, 2 * rank), jnp.float32),
            pltpu.VMEM((len(MERGED), 4 * blocks // chunks * rank, 2 * rank), jnp.bfloat16),
            pltpu.VMEM((len(MERGED), rank, LANES), jnp.float32),
            pltpu.VMEM((groups, len(MERGED), share, LANES), jnp.float32),
            pltpu.SemaphoreType.DMA((chunks // 2,)),
            pltpu.SemaphoreType.DMA((LEVELS,)),
            pltpu.SemaphoreType.DMA((LEVELS, chunks)),
            pltpu.SemaphoreType.DMA((LEVELS, chunks)),
            pltpu.SemaphoreType.DMA((groups - 1, chunks)),
            pltpu.SemaphoreType.DMA((groups - 1, chunks)),
            pltpu.SemaphoreType.REGULAR((LEVELS - 1 + 2 * (groups - 1),)),
            pltpu.SemaphoreType.DMA((2, len(MERGED))),
            pltpu.SemaphoreType.DMA((groups, len(MERGED))),
            pltpu.SemaphoreType.DMA((groups, len(MERGED))),
        ],
        compiler_params=pltpu.CompilerParams(
            collective_id=0, has_side_effects=True, vmem_limit_bytes=56460000
        ),
    )(coefficients, factors)


def solution(mesh):
    placed = (P("src", None, None, "bis"), P("src", None, "bis", None, None))
    return jax.shard_map(
        per_device, mesh=mesh, in_specs=placed, out_specs=P(None, "src", "bis"), check_vma=False
    )
```

```python
import functools

import jax
import jax.numpy as jnp
from jax import lax
from jax.experimental import pallas as pl
from jax.experimental.pallas import tpu as pltpu
from jax.sharding import PartitionSpec as P

LEVELS = 3
MESH = pl.DeviceIdType.MESH
LANES = 128
HALF = LANES // 2
MERGED = (2, 3)


def flipped(index, step):
    return index + step - 2 * step * ((index // step) % 2)


def turned(packed, low_half):
    moved = pltpu.roll(packed, HALF, 1)
    return jnp.where(low_half, -moved, moved)


def kernel(steps, groups, rank, blocks, per_block,
           coef, fac, out,
           start, fbuf, fsplit, recv, state, shares, far_factors, fmerged, far_state, far_shares,
           coef_sem, fac_sem, send_sem, recv_sem, share_send, share_recv, ready, factor_sem, far_send, far_recv):
    chunks = blocks * per_block // HALF
    chunk_blocks = blocks // chunks
    rows = chunk_blocks * rank
    bis = lax.axis_index("bis")
    src = lax.axis_index("src")
    share = rank // groups
    partners = [flipped(bis, step) for step in steps]
    peers = []
    for k in range(1, groups):
        peer = src
        for bit in range(groups.bit_length() - 1):
            if (k >> bit) & 1:
                peer = flipped(peer, 1 << bit)
        peers.append(peer)

    coef_copies = []
    for half in range(chunks // 2):
        columns = pl.ds(half * LANES, LANES)
        coef_copies.append(pltpu.make_async_copy(coef.at[0, :, :, columns], start.at[:, :, columns], coef_sem.at[half]))
        coef_copies[-1].start()
    waits = [bis // steps[1] % 2, bis // steps[2] % 2]
    links = [{"bis": partners[1]}, {"bis": partners[2]}]
    for k in range(1, groups):
        waits.append(src // 2 % 2 if k >= 2 else 1 - src % 2)
        links.append({"src": peers[k - 1]})
    for k in range(1, groups):
        waits.append(bis // steps[2] % 2)
        links.append({"bis": partners[2], "src": peers[k - 1]})
    def first_device(link):
        return jnp.logical_and(link.get("bis", bis) == 0, link.get("src", src) == 0)

    me_first = first_device({})
    waits = [
        jnp.where(me_first, 1, jnp.where(first_device(link), 0, late)) for late, link in zip(waits, links)
    ]
    barrier = pltpu.get_barrier_semaphore()
    pl.semaphore_signal(barrier, inc=1, device_id={"bis": partners[0]}, device_id_type=MESH)
    for late, link in zip(waits, links):
        @pl.when(late == 0)
        def _(link=link):
            pl.semaphore_signal(barrier, inc=1, device_id=link, device_id_type=MESH)
    pl.semaphore_wait(barrier, 1 + sum(waits))

    def answered(i):
        @pl.when(waits[i] == 0)
        def _():
            pl.semaphore_wait(ready.at[i], 1)

    for i, (late, link) in enumerate(zip(waits, links)):
        @pl.when(late == 1)
        def _(i=i, link=link):
            pl.semaphore_signal(ready.at[i], inc=1, device_id=link, device_id_type=MESH)

    fac_copies = [
        pltpu.make_async_copy(fac.at[0, l], fbuf.at[l], fac_sem.at[l]) for l in range(LEVELS)
    ]
    for copy in fac_copies:
        copy.start()


    def exchange(level, chunk):
        return pltpu.make_async_remote_copy(
            src_ref=state.at[level, chunk],
            dst_ref=recv.at[level, chunk],
            send_sem=send_sem.at[level, chunk],
            recv_sem=recv_sem.at[level, chunk],
            device_id={"bis": partners[level]},
            device_id_type=MESH,
        )

    def share_copy(k, chunk):
        return pltpu.make_async_remote_copy(
            src_ref=state.at[LEVELS, chunk, pl.ds(pl.multiple_of(peers[k] * share, share), share), :],
            dst_ref=shares.at[k, chunk],
            send_sem=share_send.at[k, chunk],
            recv_sem=share_recv.at[k, chunk],
            device_id={"src": peers[k]},
            device_id_type=MESH,
        )

    far_copies = []
    for chunk in MERGED:
        index = (chunk - MERGED[0]) * chunk_blocks
        far_copies.append(
            pltpu.make_async_remote_copy(
                src_ref=fac.at[0, LEVELS - 1, pl.ds(chunk * chunk_blocks, chunk_blocks), :, pl.ds(2 * rank, 2 * rank)],
                dst_ref=far_factors.at[pl.ds(index, chunk_blocks)],
                send_sem=factor_sem.at[0, chunk - MERGED[0]],
                recv_sem=factor_sem.at[1, chunk - MERGED[0]],
                device_id={"bis": partners[LEVELS - 1]},
                device_id_type=MESH,
            )
        )

    def far_share(k, chunk):
        peer = peers[k - 1] if k else src
        link = {"bis": partners[LEVELS - 1], "src": peer} if k else {"bis": partners[LEVELS - 1]}
        return pltpu.make_async_remote_copy(
            src_ref=far_state.at[chunk - MERGED[0], pl.ds(pl.multiple_of(peer * share, share), share), :],
            dst_ref=far_shares.at[k, chunk - MERGED[0]],
            send_sem=far_send.at[k, chunk - MERGED[0]],
            recv_sem=far_recv.at[k, chunk - MERGED[0]],
            device_id=link,
            device_id_type=MESH,
        )

    low_half = lax.broadcasted_iota(jnp.int32, (rank, LANES), 1) < HALF
    lane_block = lax.broadcasted_iota(jnp.int32, (rank, LANES), 1) % HALF // per_block

    def packed(pair, chunk):
        real, imag = pair
        if chunk % 2 == 0:
            imag = pltpu.roll(imag, HALF, 1)
        else:
            real = pltpu.roll(real, HALF, 1)
        return jnp.where(low_half, real, imag)

    for chunk in range(chunks):
        tile = chunk // 2 * LANES
        if chunk % 2 == 0:
            coef_copies[chunk // 2].wait()
        state[0, chunk] = packed((start[0, :, tile:tile + LANES], start[1, :, tile:tile + LANES]), chunk)
        exchange(0, chunk).start()

    @pl.when(waits[1] == 1)
    def _():
        for copy in far_copies:
            copy.start()


    for level in range(LEVELS):
        fac_copies[level].wait()

        def split_block(block, carry, level=level):
            value = fbuf[level, block]
            high = value.astype(jnp.bfloat16)
            low = (value - high.astype(jnp.float32)).astype(jnp.bfloat16)
            chunk = block // chunk_blocks
            row = pl.multiple_of(block % chunk_blocks * rank, rank)
            fsplit[level, chunk, pl.ds(row, rank), :] = high
            fsplit[level, chunk, pl.ds(row + rows, rank), :] = low
            return carry

        if level < LEVELS - 1:
            lax.fori_loop(0, blocks, split_block, 0)
        else:
            lax.fori_loop(0, MERGED[0] * chunk_blocks, split_block, 0)

    def split_merged(block, far):
        value = far_factors[block] if far else fbuf[LEVELS - 1, MERGED[0] * chunk_blocks + block, :, :2 * rank]
        high = value.astype(jnp.bfloat16)
        low = (value - high.astype(jnp.float32)).astype(jnp.bfloat16)
        chunk = block // chunk_blocks
        row = pl.multiple_of(block % chunk_blocks * rank, rank) + far * rows
        fmerged[chunk, pl.ds(row, rank), :] = high
        fmerged[chunk, pl.ds(row + 2 * rows, rank), :] = low

    def split_near(block, carry):
        split_merged(block, 0)
        return carry

    def split_far(block, carry):
        split_merged(block, 1)
        return carry

    lax.fori_loop(0, len(MERGED) * chunk_blocks, split_near, 0)

    def merged(chunk, value):
        index = chunk - MERGED[0]
        weights = jnp.concatenate([value, turned(value, low_half)], axis=0)
        high = weights.astype(jnp.bfloat16)
        low = (weights - high.astype(jnp.float32)).astype(jnp.bfloat16)
        product = jnp.dot(
            fmerged[index, :2 * rows], jnp.concatenate([high, low], axis=1), preferred_element_type=jnp.float32
        )
        summed = product[:, :LANES] + product[:, LANES:] + jnp.dot(
            fmerged[index, 2 * rows:], high, preferred_element_type=jnp.float32
        )
        for far in (1, 0):
            picked = summed[far * rows:far * rows + rank]
            for b in range(1, chunk_blocks):
                picked = jnp.where(lane_block == b, summed[far * rows + b * rank:far * rows + (b + 1) * rank], picked)
            if far:
                far_state[index] = picked
            else:
                state[LEVELS, chunk] = picked
        for k in range(groups):
            if chunk == MERGED[0] and k:
                answered(LEVELS - 1 + groups - 1 + k - 1)
            far_share(k, chunk).start()
        for k in range(groups - 1):
            if chunk == MERGED[0]:
                answered(LEVELS - 1 + k)
            share_copy(k, chunk).start()

    def step(level, chunk):
        own = state[level, chunk]
        exchange(level, chunk).wait_recv()
        other = recv[level, chunk]
        weights = jnp.concatenate([own, turned(own, low_half), other, turned(other, low_half)], axis=0)
        high = weights.astype(jnp.bfloat16)
        low = (weights - high.astype(jnp.float32)).astype(jnp.bfloat16)
        fh = fsplit[level, chunk, :rows]
        fl = fsplit[level, chunk, rows:]
        product = jnp.dot(fh, jnp.concatenate([high, low], axis=1), preferred_element_type=jnp.float32)
        summed = product[:, :LANES] + product[:, LANES:] + jnp.dot(fl, high, preferred_element_type=jnp.float32)
        picked = summed[0:rank]
        for b in range(1, chunk_blocks):
            picked = jnp.where(lane_block == b, summed[b * rank:(b + 1) * rank], picked)
        if level == LEVELS - 2 and chunk in MERGED:
            merged(chunk, picked)
            return
        state[level + 1, chunk] = picked
        if level + 1 < LEVELS:
            if chunk == 0 and level == 0:
                answered(0)
            exchange(level + 1, chunk).start()
        else:
            for k in range(groups - 1):
                share_copy(k, chunk).start()

    for level in range(LEVELS):
        for chunk in range(chunks if level < LEVELS - 1 else MERGED[0]):
            if level == LEVELS - 2 and chunk in MERGED:
                index = chunk - MERGED[0]
                far_copies[index].wait_recv()
                lax.fori_loop(index * chunk_blocks, (index + 1) * chunk_blocks, split_far, 0)
            step(level, chunk)
            if level == 0 and chunk == 0:
                @pl.when(waits[1] == 0)
                def _():
                    pl.semaphore_wait(ready.at[1], 1)
                    for copy in far_copies:
                        copy.start()

    own_rows = pl.ds(pl.multiple_of(src * share, share), share)
    low_share = lax.broadcasted_iota(jnp.int32, (share, LANES), 1) < HALF
    for pair in reversed(range(chunks // 2)):
        totals = []
        for chunk in (2 * pair, 2 * pair + 1):
            total = state[LEVELS, chunk, own_rows, :]
            for k in range(groups - 1):
                share_copy(k, chunk).wait_recv()
                total = total + shares[k, chunk]
            if chunk in MERGED:
                for k in range(groups):
                    far_share(k, chunk).wait_recv()
                    total = total + far_shares[k, chunk - MERGED[0]]
            totals.append(total)
        tile = pair * LANES
        out[0, :, tile:tile + LANES] = jnp.where(low_share, totals[0], pltpu.roll(totals[1], HALF, 1))
        out[1, :, tile:tile + LANES] = jnp.where(low_share, pltpu.roll(totals[0], HALF, 1), totals[1])
    for level in range(LEVELS):
        for chunk in range(chunks):
            if level < LEVELS - 1 or chunk not in MERGED:
                exchange(level, chunk).wait_send()
    for copy in far_copies:
        copy.wait_send()
    for chunk in MERGED:
        for k in range(groups):
            far_share(k, chunk).wait_send()
    for chunk in range(chunks):
        for k in range(groups - 1):
            share_copy(k, chunk).wait_send()


def per_device(coefficients, factors):
    middle = (lax.axis_size("bis").bit_length() - 1) // 2
    groups = lax.axis_size("src")
    _, _, rank, columns = coefficients.shape
    blocks = factors.shape[2]
    chunks = columns // HALF
    share = rank // groups
    steps = [2 ** (middle + 1 - l) for l in range(LEVELS)]
    body = functools.partial(kernel, steps, groups, rank, blocks, columns // blocks)
    return pl.pallas_call(
        body,
        out_shape=jax.ShapeDtypeStruct((2, share, columns), jnp.float32),
        in_specs=[pl.BlockSpec(memory_space=pl.ANY)] * 2,
        out_specs=pl.BlockSpec(memory_space=pltpu.VMEM),
        scratch_shapes=[
            pltpu.VMEM((2, rank, columns), jnp.float32),
            pltpu.VMEM((LEVELS, blocks, rank, 4 * rank), jnp.float32),
            pltpu.VMEM((LEVELS, chunks, 2 * blocks // chunks * rank, 4 * rank), jnp.bfloat16),
            pltpu.VMEM((LEVELS, chunks, rank, LANES), jnp.float32),
            pltpu.VMEM((LEVELS + 1, chunks, rank, LANES), jnp.float32),
            pltpu.VMEM((groups - 1, chunks, share, LANES), jnp.float32),
            pltpu.VMEM((len(MERGED) * blocks // chunks, rank, 2 * rank), jnp.float32),
            pltpu.VMEM((len(MERGED), 4 * blocks // chunks * rank, 2 * rank), jnp.bfloat16),
            pltpu.VMEM((len(MERGED), rank, LANES), jnp.float32),
            pltpu.VMEM((groups, len(MERGED), share, LANES), jnp.float32),
            pltpu.SemaphoreType.DMA((chunks // 2,)),
            pltpu.SemaphoreType.DMA((LEVELS,)),
            pltpu.SemaphoreType.DMA((LEVELS, chunks)),
            pltpu.SemaphoreType.DMA((LEVELS, chunks)),
            pltpu.SemaphoreType.DMA((groups - 1, chunks)),
            pltpu.SemaphoreType.DMA((groups - 1, chunks)),
            pltpu.SemaphoreType.REGULAR((LEVELS - 1 + 2 * (groups - 1),)),
            pltpu.SemaphoreType.DMA((2, len(MERGED))),
            pltpu.SemaphoreType.DMA((groups, len(MERGED))),
            pltpu.SemaphoreType.DMA((groups, len(MERGED))),
        ],
        compiler_params=pltpu.CompilerParams(
            collective_id=0, has_side_effects=True, vmem_limit_bytes=56460000
        ),
    )(coefficients, factors)


def solution(mesh):
    placed = (P("src", None, None, "bis"), P("src", None, "bis", None, None))
    return jax.shard_map(
        per_device, mesh=mesh, in_specs=placed, out_specs=P(None, "src", "bis"), check_vma=False
    )
```
